32 devices in a mesh: tm: 8 (over y, x, core), orb: 4 (over z).
Axes of the slice: x: 2, y: 2, z: 4, core: 2. Of those that a mesh axis runs over, the one named last changes fastest.
Arguments:
- greater: bfloat16 [16, 2048, 2048], P('tm', 'orb'), may hold values from -6 to 6
- lesser_back: bfloat16 [16, 2048, 2048], P('tm', 'orb'), may hold values from -6 to 6
- coupling: bfloat16 [2048, 2048], P('orb'), may hold values from -0.25 to 0.25
- pattern: int32 [16, 16], replicated, may hold values 0 or 1
- rates: float32 [2048], replicated, may hold values from 0.05 to 1
- density_now: bfloat16 [2048, 2048], P('orb'), may hold values from -6 to 6
- time_step: float32 [1], replicated, may hold values from 0.1 to 0.25
Outputs:
- new_lesser: bfloat16 [16, 2048, 2048], P('tm', 'orb')
- density: bfloat16 [2048, 2048], P('orb')
The draws below stay inside these ranges and needn't reach their ends.
All inputs are finite; a program needn't handle non-finite values.
Results may differ from the reference program's by a relative error of at most 0.006.
Values may be sent and summed in bfloat16 or wider, within the bound.
No kernel may reach another device: no remote copies, remote signals or barrier semaphores. Data moves between devices by JAX's collectives and lax.ppermute only.
A program may use at most 128 MiB of HBM per device.

```python
import math
import jax
import jax.numpy as jnp
from jax import lax

ORBITALS = 2048
BLOCK = 128
BLOCKS = 16
TIMES = 16


def with_ends(result, rng, least, high):
    longest = result.shape.index(max(result.shape))
    spots = []
    for shift in (0, 1):
        where = [jax.random.randint(jax.random.fold_in(rng, axis), (), 0, length) for axis, length in enumerate(result.shape)]
        where[longest] = (where[longest] + shift) % result.shape[longest]
        spots.append(tuple(where))
    return result.at[spots[0]].set(least).at[spots[1]].set(high)


def block_scale(key, extent, pieces, least, largest):
    def one(axis_at, parts):
        heights = jax.random.uniform(jax.random.fold_in(jax.random.fold_in(key, 6), axis_at), (parts,), jnp.float32, least / len(pieces), largest / len(pieces))
        return jnp.repeat(jnp.exp(heights), extent[axis_at] // parts).reshape((-1,) + (1,) * (len(extent) - axis_at - 1))

    level = one(*pieces[0])
    for cut in pieces[1:]:
        level = level * one(*cut)
    return level


def gaussian(stream_key, shape, spread, limit, cuts=(), held_as=jnp.bfloat16):
    drawn = jax.random.normal(stream_key, shape, jnp.float32) * spread
    if len(cuts) > 0:
        drawn = block_scale(stream_key, shape, cuts, -0.22, 0.18) * drawn
    return jnp.clip(drawn, min=-limit, max=limit).astype(held_as)


def setup_inputs(seed: int = 0) -> dict:
    keys = jax.random.split(jax.random.key(seed), 8)
    greater = gaussian(keys[0], (TIMES, ORBITALS, ORBITALS), 1.0, 6.0, ((0, 8), (1, 4)))
    lesser_back = gaussian(keys[1], (TIMES, ORBITALS, ORBITALS), 1.0, 6.0, ((0, 8), (1, 4)))
    coupling = gaussian(keys[2], (ORBITALS, ORBITALS), (3 * ORBITALS // 10) ** -0.5, 0.25, ((0, 4),))
    pattern = with_ends((jax.random.randint(keys[3], (BLOCKS, BLOCKS), 0, 10) < 3).astype(jnp.int32), jax.random.fold_in(keys[3], 1), 0, 1)
    rates = jnp.clip(jnp.exp(jax.random.uniform(keys[4], (ORBITALS,), jnp.float32, math.log(0.05), math.log(1.0))), 0.05, 1.0)
    density_now = gaussian(keys[5], (ORBITALS, ORBITALS), 1.0, 6.0, ((0, 4),))
    time_step = jnp.clip(jnp.exp(jax.random.uniform(keys[6], (1,), jnp.float32, math.log(0.1), math.log(0.25))), 0.1, 0.25)
    return dict(greater=greater, lesser_back=lesser_back, coupling=coupling, pattern=pattern, rates=rates, density_now=density_now, time_step=time_step)


def reference(greater, lesser_back, coupling, pattern, rates, density_now, time_step):
    step_size = time_step[0]
    block_ids = jnp.arange(ORBITALS) // BLOCK
    onehot = (block_ids[:, None] == jnp.arange(BLOCKS)[None, :]).astype(jnp.float32)
    expand = jnp.dot(jnp.dot(onehot, pattern.astype(jnp.float32), precision=lax.Precision.HIGHEST), onehot.T, precision=lax.Precision.HIGHEST)
    coupling_full = (coupling.astype(jnp.float32) * expand).astype(jnp.bfloat16)
    decay_rates = rates[:, None] + rates[None, :]

    def advance(running, time_pair):
        greater_block, back_block = time_pair
        turned = back_block.T.astype(jnp.float32)
        bubble = (greater_block.astype(jnp.float32) * turned).astype(jnp.bfloat16)
        half_screened = jnp.dot(bubble, coupling_full.T, preferred_element_type=jnp.float32).astype(jnp.bfloat16)
        screened = jnp.dot(coupling_full, half_screened, preferred_element_type=jnp.float32).astype(jnp.bfloat16)
        self_energy = greater_block.astype(jnp.float32) * screened.astype(jnp.float32)
        slope_now = self_energy + decay_rates * turned
        predicted = -turned + step_size * slope_now
        renewed = -turned + 0.5 * step_size * (slope_now + self_energy - decay_rates * predicted)
        return running + self_energy * turned, renewed.astype(jnp.bfloat16)

    summed, new_lesser = lax.scan(advance, jnp.zeros((ORBITALS, ORBITALS), jnp.float32), (greater, lesser_back))
    collision = step_size * summed
    density_old = density_now.astype(jnp.float32)
    slope_old = -decay_rates * density_old
    guess = density_old + step_size * slope_old + collision
    density = density_old + 0.5 * step_size * (slope_old - decay_rates * guess) + collision
    return new_lesser, density.astype(jnp.bfloat16)
```

```python
import functools

import jax
import jax.numpy as jnp
from jax import lax
from jax.experimental import pallas as pl
from jax.experimental.pallas import tpu as pltpu
from jax.sharding import PartitionSpec as P


F32 = jnp.float32
BF16 = jnp.bfloat16


def power_of_two(number):
    return number & (number - 1) == 0


def orbit(size):
    me = lax.axis_index("orb")
    if power_of_two(size):
        pairs = [[(i, i ^ k) for i in range(size)] for k in range(size)]
        return pairs, [me ^ k for k in range(size)], [me ^ k for k in range(size)]
    pairs = [[(i, (i + k) % size) for i in range(size)] for k in range(size)]
    return pairs, [(me + k) % size for k in range(size)], [(me - k) % size for k in range(size)]


def far_first(size):
    return sorted(range(1, size), key=lambda k: (k < 2, k))


def flip(value, bit):
    size = lax.axis_size("tm")
    return lax.ppermute(value, "tm", [(i, i ^ bit) for i in range(size)])


def spread_blocks(pattern, orbitals):
    return jnp.repeat(pattern.astype(F32), orbitals // pattern.shape[0], axis=1)


def assemble_kernel(order, block, table, mask_ref, own_ref, near_ref, far_ref, out_ref):
    step = pl.program_id(0)
    size = out_ref.shape[0]
    rows = near_ref.shape[1]
    count = len(order)
    piece = min(rows, block)
    start = table[step] * size
    mine = table[pl.num_programs(0)]

    def put(value, offset):
        keep = mask_ref[pl.ds((start + offset) // block, 1), :]
        spot = pl.ds(pl.multiple_of(offset, piece), piece)
        out_ref[spot, :] = (value.astype(F32) * keep).astype(BF16)

    @pl.when(step == 0)
    def _():
        for offset in range(0, size, piece):
            put(own_ref[pl.ds(offset, piece), :], offset)

    @pl.when(step > 0)
    def _():
        for spot, relative in enumerate(order):
            source = near_ref if spot < count // 2 else far_ref
            base = (mine ^ relative) * rows
            for inner in range(0, rows, piece):
                put(source[spot % (count // 2), pl.ds(inner, piece), :], base + inner)


def assemble(table, mask, coupling, near, far, order, block):
    slab, orbitals = coupling.shape
    steps = orbitals // slab
    half, _, rows, _ = near.shape
    gathered = pl.BlockSpec(
        (half, None, rows, orbitals), lambda s, t: (0, jnp.maximum(s - 1, 0), 0, 0)
    )
    return pl.pallas_call(
        functools.partial(assemble_kernel, order, block),
        out_shape=jax.ShapeDtypeStruct((orbitals, orbitals), BF16),
        grid_spec=pltpu.PrefetchScalarGridSpec(
            num_scalar_prefetch=1,
            grid=(steps,),
            in_specs=[
                pl.BlockSpec(mask.shape, lambda s, t: (0, 0)),
                pl.BlockSpec((slab, orbitals), lambda s, t: (0, 0)),
                gathered,
                gathered,
            ],
            out_specs=pl.BlockSpec((slab, orbitals), lambda s, t: (t[s], 0)),
        ),
        cost_estimate=pl.CostEstimate(
            flops=orbitals * orbitals, bytes_accessed=4 * orbitals * orbitals, transcendentals=0
        ),
        name="assemble",
    )(table, mask, coupling, near, far)


def gather_coupling(coupling, pattern, pairs, source):
    slab, orbitals = coupling.shape
    size, members = len(pairs), lax.axis_size("tm")
    block = orbitals // pattern.shape[0]
    parts = 1
    while power_of_two(members) and parts * 2 <= members and slab % (parts * 32) == 0:
        parts *= 2
    me = lax.axis_index("tm") % parts
    rows = slab // parts
    piece = lax.dynamic_slice_in_dim(coupling, me * rows, rows, 0)
    arrived = {}
    with jax.named_scope("coupling_orb"):
        for k in far_first(size):
            arrived[k] = lax.ppermute(piece, "orb", pairs[k])
    held = jnp.stack([arrived[k] for k in range(1, size)])[None]
    order = [0]
    bit = parts // 2
    while bit > 1:
        with jax.named_scope(f"coupling_tm{bit}"):
            held = jnp.concatenate([held, flip(held, bit)], axis=0)
        order = order + [q ^ bit for q in order]
        bit //= 2
    with jax.named_scope("coupling_tm1"):
        other = flip(held, 1)
    order = order + [q ^ 1 for q in order]
    table = jnp.stack(source + [me]).astype(jnp.int32)
    return assemble(table, spread_blocks(pattern, orbitals), coupling, held, other, order, block)


def half_kernel(count, table, greater_ref, own_ref, *refs):
    arrived = refs[: count - 1]
    coupling_ref = refs[count - 1]
    turned_ref = refs[count]
    halves = refs[count + 1 : 2 * count + 1]
    bubble = refs[2 * count + 1]
    step = pl.program_id(0)
    slab = own_ref.shape[0]
    for k in range(count):

        @pl.when(step == k)
        def _(k=k):
            block = own_ref if k == 0 else arrived[k - 1]
            turned = block[...].T
            turned_ref[...] = turned
            product = greater_ref[...].astype(F32) * turned.astype(F32)
            spot = pl.ds(pl.multiple_of(table[k] * slab, slab), slab)
            bubble[:, spot] = product.astype(BF16)

        @pl.when(step == count + k)
        def _(k=k):
            halves[k][...] = lax.dot_general(
                bubble[...], coupling_ref[...], (((1,), (1,)), ((), ())), preferred_element_type=F32
            ).astype(BF16)


def half_screen(time, table, greater, lesser_back, arrived, coupling_full):
    _, slab, orbitals = greater.shape
    count = orbitals // slab
    whole = pl.BlockSpec((slab, slab), lambda s, t: (0, 0))
    outs = pl.pallas_call(
        functools.partial(half_kernel, count),
        out_shape=[jax.ShapeDtypeStruct((slab, orbitals), BF16)]
        + [jax.ShapeDtypeStruct((slab, slab), BF16)] * count,
        grid_spec=pltpu.PrefetchScalarGridSpec(
            num_scalar_prefetch=1,
            grid=(2 * count,),
            in_specs=[
                pl.BlockSpec(
                    (None, slab, slab), lambda s, t: (time, 0, t[jnp.minimum(s, count - 1)])
                ),
                pl.BlockSpec((None, slab, slab), lambda s, t: (time, 0, t[0])),
            ]
            + [whole] * (count - 1)
            + [
                pl.BlockSpec(
                    (slab, orbitals), lambda s, t: (t[count + jnp.maximum(s - count, 0)], 0)
                )
            ],
            out_specs=[
                pl.BlockSpec((slab, slab), lambda s, t: (0, t[jnp.minimum(s, count - 1)]))
            ]
            + [whole] * count,
            scratch_shapes=[pltpu.VMEM((slab, orbitals), BF16)],
        ),
        cost_estimate=pl.CostEstimate(
            flops=2 * slab * orbitals * orbitals,
            bytes_accessed=2 * orbitals * orbitals + 8 * slab * orbitals,
            transcendentals=0,
        ),
        name="half_screen",
    )(table, greater, lesser_back, *arrived, coupling_full)
    return outs[0], outs[1:]


def screen_kernel(count, chunks, table, *refs):
    blocks = refs[:count]
    coupling_ref = refs[count]
    outs = refs[count + 1 : count + 1 + count * len(chunks)]
    columns = refs[-1]
    step = pl.program_id(0)
    slab = blocks[0].shape[0]

    @pl.when(step == 0)
    def _():
        for k in range(count):
            columns[pl.ds(pl.multiple_of(table[k] * slab, slab), slab), :] = blocks[k][...]

    for k in range(count):

        @pl.when(step == (k - 1) % count)
        def _(k=k):
            product = jnp.dot(coupling_ref[...], columns[...], preferred_element_type=F32)
            for c, (start, rows) in enumerate(chunks):
                outs[k * len(chunks) + c][...] = product[start : start + rows, :].astype(BF16)


def screen(table, blocks, coupling_full, chunks):
    count = len(blocks)
    slab = blocks[0].shape[0]
    orbitals = coupling_full.shape[0]
    outs = pl.pallas_call(
        functools.partial(screen_kernel, count, chunks),
        out_shape=[jax.ShapeDtypeStruct((rows, slab), BF16) for _ in range(count) for _, rows in chunks],
        grid_spec=pltpu.PrefetchScalarGridSpec(
            num_scalar_prefetch=1,
            grid=(count,),
            in_specs=[pl.BlockSpec((slab, slab), lambda s, t: (0, 0))] * count
            + [pl.BlockSpec((slab, orbitals), lambda s, t: (t[count + (s + 1) % count], 0))],
            out_specs=[
                pl.BlockSpec((rows, slab), lambda s, t: (0, 0)) for _ in range(count) for _, rows in chunks
            ],
            scratch_shapes=[pltpu.VMEM((orbitals, slab), BF16)],
        ),
        cost_estimate=pl.CostEstimate(
            flops=2 * slab * orbitals * orbitals,
            bytes_accessed=2 * orbitals * orbitals + 4 * slab * orbitals,
            transcendentals=0,
        ),
        name="screen",
    )(table, *blocks, coupling_full)
    return [[outs[k * len(chunks) + c] for k in range(count)] for c in range(len(chunks))]


def renew_kernel(count, carried, table, step_ref, row_ref, column_ref, greater_ref, turned_ref, *refs):
    blocks = refs[:count]
    rest = refs[count:]
    new_ref, sum_ref = rest[-2:]
    step = pl.program_id(0)
    size = step_ref[0]
    for k in range(count):

        @pl.when(step == k)
        def _(k=k):
            greater = greater_ref[...].astype(F32)
            turned = turned_ref[...].astype(F32)
            energy = greater * blocks[k][...].astype(F32)
            decay = row_ref[...] + column_ref[...]
            slope = energy + decay * turned
            predicted = -turned + size * slope
            new = -turned + 0.5 * size * (slope + energy - decay * predicted)
            new_ref[...] = new.astype(BF16)
            part = energy * turned
            if carried:
                part = part + rest[0][...]
            sum_ref[...] = part.astype(sum_ref.dtype)


def renew(time, chunk, table, step_size, row_rates, rates, greater, turned, blocks, partial, target, kind):
    start, rows = chunk
    _, slab, orbitals = greater.shape
    count = len(blocks)
    at = start // rows
    extra, extra_specs, alias = [], [], {}
    if partial is not None:
        extra.append(partial)
        extra_specs.append(pl.BlockSpec((rows, slab), lambda s, t: (at, t[s])))
    if target is not None:
        extra.append(target)
        extra_specs.append(pl.BlockSpec(memory_space=pl.ANY))
        alias = {6 + count + len(extra) - 1: 0}
    return pl.pallas_call(
        functools.partial(renew_kernel, count, partial is not None),
        out_shape=[
            jax.ShapeDtypeStruct(greater.shape, BF16),
            jax.ShapeDtypeStruct((rows, orbitals), kind),
        ],
        grid_spec=pltpu.PrefetchScalarGridSpec(
            num_scalar_prefetch=1,
            grid=(count,),
            in_specs=[
                pl.BlockSpec(memory_space=pltpu.SMEM),
                pl.BlockSpec((rows, 1), lambda s, t: (at, 0)),
                pl.BlockSpec((1, slab), lambda s, t: (0, t[s])),
                pl.BlockSpec((None, rows, slab), lambda s, t: (time, at, t[s])),
                pl.BlockSpec((rows, slab), lambda s, t: (at, t[s])),
            ]
            + [pl.BlockSpec((rows, slab), lambda s, t: (0, 0))] * count
            + extra_specs,
            out_specs=[
                pl.BlockSpec((None, rows, slab), lambda s, t: (time, at, t[s])),
                pl.BlockSpec((rows, slab), lambda s, t: (0, t[s])),
            ],
        ),
        input_output_aliases=alias,
        cost_estimate=pl.CostEstimate(
            flops=16 * rows * orbitals, bytes_accessed=12 * rows * orbitals, transcendentals=0
        ),
        name="renew",
    )(table, step_size, row_rates, rates[None, :], greater, turned, *blocks, *extra)


def total(part):
    members = lax.axis_size("tm")
    if not power_of_two(members):
        return lax.psum(part.astype(F32), "tm")
    bit = 1
    value = part.astype(F32)
    while bit < members:
        rounded = value.astype(BF16)
        value = rounded.astype(F32) + flip(rounded, bit).astype(F32)
        bit *= 2
    return value


def row_chunks(slab):
    sizes = [slab // 4] * 3 + [slab // 8] + [slab // 16] * 2
    while min(sizes) < 16 and len(sizes) > 1:
        last = sizes.pop()
        sizes[-1] += last
    chunks, start = [], 0
    for size in sizes:
        chunks.append((start, size))
        start += size
    if any(start % size for start, size in chunks):
        return [(0, slab)]
    return chunks


def advance_density(density_old, collision, decay_rates, step_size):
    slope_old = -decay_rates * density_old
    guess = density_old + step_size * slope_old + collision
    return density_old + 0.5 * step_size * (slope_old - decay_rates * guess) + collision


def shards(greater, lesser_back, coupling, pattern, rates, density_now, time_step):
    times, slab, orbitals = greater.shape
    size = orbitals // slab
    pairs, target, source = orbit(size)
    table = jnp.stack(source + target).astype(jnp.int32)
    row_rates = lax.dynamic_slice_in_dim(rates, source[0] * slab, slab)

    def trade(name, blocks):
        arrived = {}
        with jax.named_scope(name):
            for k in far_first(size):
                arrived[k] = lax.ppermute(blocks[k], "orb", pairs[k])
        return [arrived[k] for k in range(1, size)]

    back = []
    for t in range(times):
        blocks = [None] + [
            lax.dynamic_slice(lesser_back[t], (0, target[k] * slab), (slab, slab)) for k in range(1, size)
        ]
        back.append(trade(f"back{t}", blocks))
    coupling_full = gather_coupling(coupling, pattern, pairs, source)
    turned, halves = [], []
    for t in range(times):
        one, blocks = half_screen(t, table, greater, lesser_back, back[t], coupling_full)
        turned.append(one)
        halves.append([blocks[0]] + trade(f"half{t}", blocks))
    new_lesser, partial, parts = None, None, []
    chunks = row_chunks(slab)
    for t in range(times):
        last = t == times - 1
        pieces = chunks if last else [(0, slab)]
        columns = screen(table, halves[t], coupling_full, pieces)
        for c, piece in enumerate(pieces):
            blocks = [columns[c][0]] + trade(f"screened{t}_{c}", columns[c])
            new_lesser, part = renew(
                t, piece, table, time_step, row_rates[:, None], rates, greater, turned[t], blocks,
                partial, new_lesser, BF16 if last else F32,
            )
            if last:
                parts.append(part)
            else:
                partial = part
    step_size = time_step[0]
    rows = []
    for (start, count), part in zip(chunks, parts):
        with jax.named_scope(f"collision{start}"):
            collision = step_size * total(part)
        old = density_now[start : start + count].astype(F32)
        decay = row_rates[start : start + count, None] + rates[None, :]
        rows.append(advance_density(old, collision, decay, step_size).astype(BF16))
    return new_lesser, jnp.concatenate(rows, axis=0)


def solution(mesh):
    return jax.shard_map(
        shards,
        mesh=mesh,
        in_specs=(
            P("tm", "orb", None),
            P("tm", "orb", None),
            P("orb", None),
            P(),
            P(),
            P("orb", None),
            P(),
        ),
        out_specs=(P("tm", "orb", None), P("orb", None)),
        check_vma=False,
    )
```

```python
import functools

import jax
import jax.numpy as jnp
from jax import lax
from jax.experimental import pallas as pl
from jax.experimental.pallas import tpu as pltpu
from jax.sharding import PartitionSpec as P


F32 = jnp.float32
BF16 = jnp.bfloat16


def power_of_two(number):
    return number & (number - 1) == 0


def orbit(size):
    me = lax.axis_index("orb")
    if power_of_two(size):
        pairs = [[(i, i ^ k) for i in range(size)] for k in range(size)]
        return pairs, [me ^ k for k in range(size)], [me ^ k for k in range(size)]
    pairs = [[(i, (i + k) % size) for i in range(size)] for k in range(size)]
    return pairs, [(me + k) % size for k in range(size)], [(me - k) % size for k in range(size)]


def send(value, pairs):
    return lax.ppermute(value, "orb", pairs)


def trade(blocks, pairs):
    size = len(pairs)
    arrived = {k: send(blocks[k], pairs[k]) for k in range(1, size)}
    return [arrived[k] for k in range(1, size)]


def spread(piece, pairs):
    size = len(pairs)
    if size != 4:
        return [send(piece, pairs[k]) for k in range(1, size)]
    two = send(piece, pairs[2])
    one = send(piece, pairs[1])
    return [one, two, send(two, pairs[1])]


def flip(value, bit):
    size = lax.axis_size("tm")
    return lax.ppermute(value, "tm", [(i, i ^ bit) for i in range(size)])


def spread_blocks(pattern, orbitals):
    return jnp.repeat(pattern.astype(F32), orbitals // pattern.shape[0], axis=1)


def assemble_kernel(orders, block, table, mask_ref, own_ref, *refs):
    out_ref = refs[-1]
    step = pl.program_id(0)
    size = out_ref.shape[0]
    rows = refs[0].shape[1]
    count = len(orders[0])
    piece = min(rows, block)
    start = table[step] * size
    mine = table[pl.num_programs(0)]

    def put(value, offset):
        keep = mask_ref[pl.ds((start + offset) // block, 1), :]
        spot = pl.ds(pl.multiple_of(offset, piece), piece)
        out_ref[spot, :] = (value.astype(F32) * keep).astype(BF16)

    @pl.when(step == 0)
    def _():
        for offset in range(0, size, piece):
            put(own_ref[pl.ds(offset, piece), :], offset)

    @pl.when(step > 0)
    def _():
        for part, order in enumerate(orders):
            for spot, relative in enumerate(order):
                held = refs[2 * part + (spot >= count // 2)]
                base = ((mine ^ relative) * len(orders) + part) * rows
                for inner in range(0, rows, piece):
                    put(held[spot % (count // 2), pl.ds(inner, piece), :], base + inner)


def assemble(table, mask, coupling, gathered, orders, block):
    slab, orbitals = coupling.shape
    steps = orbitals // slab
    half, _, rows, _ = gathered[0].shape
    spec = pl.BlockSpec((half, None, rows, orbitals), lambda s, t: (0, jnp.maximum(s - 1, 0), 0, 0))
    return pl.pallas_call(
        functools.partial(assemble_kernel, orders, block),
        out_shape=jax.ShapeDtypeStruct((orbitals, orbitals), BF16),
        grid_spec=pltpu.PrefetchScalarGridSpec(
            num_scalar_prefetch=1,
            grid=(steps,),
            in_specs=[
                pl.BlockSpec(mask.shape, lambda s, t: (0, 0)),
                pl.BlockSpec((slab, orbitals), lambda s, t: (0, 0)),
            ]
            + [spec] * len(gathered),
            out_specs=pl.BlockSpec((slab, orbitals), lambda s, t: (t[s], 0)),
        ),
        cost_estimate=pl.CostEstimate(
            flops=orbitals * orbitals, bytes_accessed=4 * orbitals * orbitals, transcendentals=0
        ),
        name="assemble",
    )(table, mask, coupling, *gathered)


def share_bits(slab, members):
    parts = 1
    while power_of_two(members) and parts * 2 <= members and slab % (parts * 64) == 0:
        parts *= 2
    return parts, [1 << i for i in range(1, parts.bit_length() - 1)]


def gather_coupling(coupling, pattern, pairs, source):
    slab, orbitals = coupling.shape
    members = lax.axis_size("tm")
    block = orbitals // pattern.shape[0]
    parts, bits = share_bits(slab, members)
    me = lax.axis_index("tm") % parts
    rows = slab // parts
    piece = lax.dynamic_slice_in_dim(coupling, me * rows, rows, 0)
    held = jnp.stack(spread(piece, pairs))[None]
    gathered, orders = [], []
    for half in range(2):
        mine = held[:, :, half * (rows // 2) : (half + 1) * (rows // 2)]
        order = [0]
        for bit in bits if half else bits[::-1]:
            mine = jnp.concatenate([mine, flip(mine, bit)], axis=0)
            order = order + [q ^ bit for q in order]
        other = flip(mine, 1)
        gathered += [mine, other]
        orders.append(order + [q ^ 1 for q in order])
    table = jnp.stack(source + [me]).astype(jnp.int32)
    mask = spread_blocks(pattern, orbitals)
    return assemble(table, mask, coupling, gathered, orders, block)


def half_kernel(count, table, greater_ref, own_ref, *refs):
    arrived = refs[: count - 1]
    coupling_ref = refs[count - 1]
    turned_ref = refs[count]
    halves = refs[count + 1 : 2 * count + 1]
    bubble = refs[2 * count + 1]
    step = pl.program_id(0)
    slab = own_ref.shape[0]
    for k in range(count):

        @pl.when(step == k)
        def _(k=k):
            block = own_ref if k == 0 else arrived[k - 1]
            turned = block[...].T
            turned_ref[...] = turned
            product = greater_ref[...].astype(F32) * turned.astype(F32)
            spot = pl.ds(pl.multiple_of(table[k] * slab, slab), slab)
            bubble[:, spot] = product.astype(BF16)

        @pl.when(step == count + k)
        def _(k=k):
            halves[k][...] = lax.dot_general(
                bubble[...], coupling_ref[...], (((1,), (1,)), ((), ())), preferred_element_type=F32
            ).astype(BF16)


def half_screen(time, table, greater, lesser_back, arrived, coupling_full):
    _, slab, orbitals = greater.shape
    count = orbitals // slab
    whole = pl.BlockSpec((slab, slab), lambda s, t: (0, 0))
    outs = pl.pallas_call(
        functools.partial(half_kernel, count),
        out_shape=[jax.ShapeDtypeStruct((slab, orbitals), BF16)]
        + [jax.ShapeDtypeStruct((slab, slab), BF16)] * count,
        grid_spec=pltpu.PrefetchScalarGridSpec(
            num_scalar_prefetch=1,
            grid=(2 * count,),
            in_specs=[
                pl.BlockSpec(
                    (None, slab, slab), lambda s, t: (time, 0, t[jnp.minimum(s, count - 1)])
                ),
                pl.BlockSpec((None, slab, slab), lambda s, t: (time, 0, t[0])),
            ]
            + [whole] * (count - 1)
            + [
                pl.BlockSpec(
                    (slab, orbitals), lambda s, t: (t[count + jnp.maximum(s - count, 0)], 0)
                )
            ],
            out_specs=[
                pl.BlockSpec((slab, slab), lambda s, t: (0, t[jnp.minimum(s, count - 1)]))
            ]
            + [whole] * count,
            scratch_shapes=[pltpu.VMEM((slab, orbitals), BF16)],
        ),
        cost_estimate=pl.CostEstimate(
            flops=2 * slab * orbitals * orbitals,
            bytes_accessed=2 * orbitals * orbitals + 8 * slab * orbitals,
            transcendentals=0,
        ),
        name="half_screen",
    )(table, greater, lesser_back, *arrived, coupling_full)
    return outs[0], outs[1:]


def screen_kernel(count, chunks, earlier, table, *refs):
    blocks = refs[:count]
    coupling_ref = refs[count]
    kept = refs[count + 1 : count + 1 + earlier]
    heads = refs[count + 1 + earlier : 2 * count + 1 + earlier]
    rest = refs[2 * count + 1 + earlier : -1]
    columns = refs[-1]
    step = pl.program_id(0)
    slab = blocks[0].shape[0]
    first = chunks[0][1]

    @pl.when(step == 0)
    def _():
        for k in range(count):
            columns[pl.ds(pl.multiple_of(table[k] * slab, slab), slab), :] = blocks[k][...]

    for k in range(count):

        @pl.when(step == (k - 1) % count)
        def _(k=k):
            product = jnp.dot(coupling_ref[...], columns[...], preferred_element_type=F32).astype(BF16)
            heads[k][0] = product[:first, :]
            if len(rest) == 1:
                rest[0][k] = product[first:, :]
            for c, (start, rows) in enumerate(chunks[1:]):
                if len(rest) > 1:
                    out = rest[c * count + k]
                    for t in range(earlier):
                        out[t] = kept[t][k, start - first : start - first + rows, :]
                    out[earlier] = product[start : start + rows, :]


def screen(table, blocks, coupling_full, chunks, kept, last):
    count = len(blocks)
    slab = blocks[0].shape[0]
    orbitals = coupling_full.shape[0]
    first = chunks[0][1]
    shapes = [(1, first, slab)] * count
    if last:
        shapes += [(len(kept) + 1, rows, slab) for _, rows in chunks[1:] for _ in range(count)]
    else:
        shapes += [(count, slab - first, slab)]
    outs = pl.pallas_call(
        functools.partial(screen_kernel, count, chunks, len(kept)),
        out_shape=[jax.ShapeDtypeStruct(shape, BF16) for shape in shapes],
        grid_spec=pltpu.PrefetchScalarGridSpec(
            num_scalar_prefetch=1,
            grid=(count,),
            in_specs=[pl.BlockSpec((slab, slab), lambda s, t: (0, 0))] * count
            + [pl.BlockSpec((slab, orbitals), lambda s, t: (t[count + (s + 1) % count], 0))]
            + [pl.BlockSpec(one.shape, lambda s, t: (0, 0, 0)) for one in kept],
            out_specs=[pl.BlockSpec(shape, lambda s, t: (0, 0, 0)) for shape in shapes],
            scratch_shapes=[pltpu.VMEM((orbitals, slab), BF16)],
        ),
        cost_estimate=pl.CostEstimate(
            flops=2 * slab * orbitals * orbitals,
            bytes_accessed=2 * orbitals * orbitals + 4 * slab * orbitals,
            transcendentals=0,
        ),
        name="screen",
    )(table, *blocks, coupling_full, *kept)
    return outs[:count], outs[count:]


def renew_kernel(count, times, each, table, step_ref, row_ref, column_ref, greater_ref, *refs):
    turned_refs = refs[:times]
    new_ref, sum_ref = refs[-2:]
    blocks = refs[times : times + each * count]
    size = step_ref[0]
    slab = blocks[0].shape[2]
    for k in range(count):
        spot = pl.ds(pl.multiple_of(table[k] * slab, slab), slab)
        decay = row_ref[...] + column_ref[:, spot]
        total = None
        for t in range(times):
            greater = greater_ref[t, :, spot].astype(F32)
            turned = turned_refs[t][:, spot].astype(F32)
            energy = greater * blocks[k * each + t % each][t // each].astype(F32)
            slope = energy + decay * turned
            predicted = -turned + size * slope
            new = -turned + 0.5 * size * (slope + energy - decay * predicted)
            new_ref[t, :, spot] = new.astype(BF16)
            part = energy * turned
            total = part if total is None else total + part
        sum_ref[:, spot] = total.astype(sum_ref.dtype)


def renew(chunk, table, step_size, row_rates, rates, greater, turned, blocks, target):
    start, rows = chunk
    times, slab, orbitals = greater.shape
    count, each = len(blocks), len(blocks[0])
    tall = min(rows, 128)
    while start % tall or rows % tall:
        tall //= 2
    at = start // tall
    extra = [] if target is None else [target]
    return pl.pallas_call(
        functools.partial(renew_kernel, count, times, each),
        out_shape=[
            jax.ShapeDtypeStruct(greater.shape, BF16),
            jax.ShapeDtypeStruct((rows, orbitals), BF16),
        ],
        grid_spec=pltpu.PrefetchScalarGridSpec(
            num_scalar_prefetch=1,
            grid=(rows // tall,),
            in_specs=[
                pl.BlockSpec(memory_space=pltpu.SMEM),
                pl.BlockSpec((tall, 1), lambda s, t: (at + s, 0)),
                pl.BlockSpec((1, orbitals), lambda s, t: (0, 0)),
                pl.BlockSpec((times, tall, orbitals), lambda s, t: (0, at + s, 0)),
            ]
            + [pl.BlockSpec((tall, orbitals), lambda s, t: (at + s, 0))] * times
            + [pl.BlockSpec((times // each, tall, slab), lambda s, t: (0, s, 0))] * (each * count)
            + [pl.BlockSpec(memory_space=pl.ANY)] * len(extra),
            out_specs=[
                pl.BlockSpec((times, tall, orbitals), lambda s, t: (0, at + s, 0)),
                pl.BlockSpec((tall, orbitals), lambda s, t: (s, 0)),
            ],
        ),
        input_output_aliases={5 + times + each * count: 0} if extra else {},
        cost_estimate=pl.CostEstimate(
            flops=16 * times * rows * orbitals,
            bytes_accessed=8 * times * rows * orbitals,
            transcendentals=0,
        ),
        name="renew",
    )(
        table, step_size, row_rates, rates[None, :], greater, *turned,
        *[block for one in blocks for block in one], *extra,
    )


def rounds(value, bits):
    for bit in bits:
        rounded = value.astype(BF16)
        other = flip(rounded, bit)
        value = rounded.astype(F32) + other.astype(F32)
    return value


def row_chunks(slab):
    sizes = [slab // 2, slab // 4, 3 * slab // 16, slab // 16]
    if min(sizes) < 16:
        sizes = [slab // 2] * 2
    chunks, start = [], 0
    for size in sizes:
        chunks.append((start, size))
        start += size
    return chunks


def advance_density(density_old, collision, decay_rates, step_size):
    slope_old = -decay_rates * density_old
    guess = density_old + step_size * slope_old + collision
    return density_old + 0.5 * step_size * (slope_old - decay_rates * guess) + collision


def finish(parts, chunks, row_rates, rates, density_now, step_size):
    members = lax.axis_size("tm")
    upper = lax.axis_index("tm") % 2
    doubling = power_of_two(members)
    bits = [1 << i for i in range(members.bit_length() - 1)]

    def density(part, start, rows):
        old = lax.dynamic_slice_in_dim(density_now, start, rows, 0).astype(F32)
        decay = lax.dynamic_slice_in_dim(row_rates, start, rows)[:, None] + rates[None, :]
        return advance_density(old, step_size * part, decay, step_size).astype(BF16)

    rows = []
    for c, ((start, count), part) in enumerate(zip(chunks, parts)):
        if not doubling:
            rows.append(density(lax.psum(part.astype(F32), "tm"), start, count))
        elif c == len(chunks) - 1 or count < 64 or members < 2:
            rows.append(density(rounds(part.astype(F32), bits), start, count))
        else:
            half = count // 2
            kept = lax.dynamic_slice_in_dim(part, upper * half, half, 0)
            sent = lax.dynamic_slice_in_dim(part, (1 - upper) * half, half, 0)
            sent = flip(sent, 1)
            value = kept.astype(F32) + sent.astype(F32)
            own = density(rounds(value, bits[1:]), start + upper * half, half)
            other = flip(own, 1)
            rows.append(jnp.where(upper == 0, own, other))
            rows.append(jnp.where(upper == 0, other, own))
    return jnp.concatenate(rows, axis=0)


def body(greater, lesser_back, coupling, pattern, rates, density_now, time_step):
    times, slab, orbitals = greater.shape
    size = orbitals // slab
    pairs, target, source = orbit(size)
    table = jnp.stack(source + target).astype(jnp.int32)
    row_rates = lax.dynamic_slice_in_dim(rates, source[0] * slab, slab)

    back = []
    for t in range(times):
        blocks = [None] + [
            lax.dynamic_slice(lesser_back, (t, 0, target[k] * slab), (1, slab, slab))[0]
            for k in range(1, size)
        ]
        back.append(trade(blocks, pairs))
    coupling_full = gather_coupling(coupling, pattern, pairs, source)
    turned, halves = [], []
    for t in range(times):
        one, blocks = half_screen(t, table, greater, lesser_back, back[t], coupling_full)
        turned.append(one)
        halves.append([blocks[0]] + trade(blocks, pairs))
    chunks = row_chunks(slab)
    heads, kept = [], []
    for t in range(times):
        head, rest = screen(table, halves[t], coupling_full, chunks, kept, t == times - 1)
        heads.append([head[0]] + trade(head, pairs))
        kept = kept + list(rest)
    joined = kept[times - 1 :]
    new_lesser, parts = None, []
    for c, chunk in enumerate(chunks):
        if c == 0:
            blocks = [[heads[t][k] for t in range(times)] for k in range(size)]
        else:
            mine = joined[(c - 1) * size : c * size]
            arrived = trade(mine, pairs)
            blocks = [[one] for one in [mine[0]] + arrived]
        new_lesser, part = renew(
            chunk, table, time_step, row_rates[:, None], rates, greater, turned, blocks, new_lesser
        )
        parts.append(part)
    return new_lesser, finish(parts, chunks, row_rates, rates, density_now, time_step[0])


def solution(mesh):
    whole = jax.shard_map(
        body,
        mesh=mesh,
        in_specs=(
            P("tm", "orb", None),
            P("tm", "orb", None),
            P("orb", None),
            P(),
            P(),
            P("orb", None),
            P(),
        ),
        out_specs=(P("tm", "orb", None), P("orb", None)),
        check_vma=False,
    )

    if mesh.shape["orb"] != 4 or mesh.shape["tm"] != 8:
        return whole

    def step(greater, lesser_back, coupling, pattern, rates, density_now, time_step):
        times = greater.shape[0] // mesh.shape["tm"]
        slab = greater.shape[1] // mesh.shape["orb"]
        chunks = row_chunks(slab)
        bits = share_bits(slab, mesh.shape["tm"])[1]
        if times != 2 or len(chunks) != 4 or len(bits) != 2:
            return whole(greater, lesser_back, coupling, pattern, rates, density_now, time_step)
        inner = whole
        return inner(greater, lesser_back, coupling, pattern, rates, density_now, time_step)

    return step
```
